32 devices in a mesh: dp: 2 (over core), expert: 16 (over z, y, x).
Axes of the slice: x: 2, y: 2, z: 4, core: 2. Of those that a mesh axis runs over, the one named last changes fastest.
Arguments:
- tokens: bfloat16 [2048, 2048], P('expert'), may hold values from -6 to 6
- out_grad: bfloat16 [2048, 2048], P('expert'), may hold values from -6 to 6
- route_ids: int32 [2048, 8], P('expert'), may hold values from 0 to 15, all different within a row; in each aligned block of 128 rows (0 to 127, 128 to 255, ...) at most 72 rows name the same one
- route_probs: float32 [2048, 8], P('expert'), may hold values from 0.05 to 1
- gate_store: bfloat16 [16, 2048, 768], P(None, 'expert', 'dp'), may hold values from -0.125 to 0.125
- up_store: bfloat16 [16, 2048, 768], P(None, 'expert', 'dp'), may hold values from -0.125 to 0.125
- down_store: bfloat16 [16, 2048, 768], P(None, 'expert', 'dp'), may hold values from -0.21875 to 0.21875
Outputs:
- grad_gate: bfloat16 [16, 2048, 768], P('expert', None, 'dp')
- grad_up: bfloat16 [16, 2048, 768], P('expert', None, 'dp')
- grad_down: bfloat16 [16, 2048, 768], P('expert', None, 'dp')
- grad_tokens: bfloat16 [2048, 2048], P('expert')
The draws below stay inside these ranges and needn't reach their ends.
Inputs may be any that keep to these rules, and one draw needn't show every extreme that they name: `route_ids`: among the 128 tokens of one device no expert is named more than 72 times, and in every draw some expert is named exactly 72 times by some device's tokens.
All inputs are finite; a program needn't handle non-finite values.
Results may differ from the reference program's by a relative error of at most 0.0065.
Values may be sent and summed in bfloat16 or wider, within the bound.
A program may use at most 128 MiB of HBM per device.

```python
import math
import jax
import jax.numpy as jnp
import numpy as np
from jax import lax

D = 2048
HID = 768
TOPK = 8
TOK_DEV = 128
EXPERTS = 16
TOKENS = 2048
CAP = 72
N_EXPERT = 16


def levels(rng, shape, cuts, least, top_value):
    def one(dim, blocks):
        steps = jax.random.uniform(jax.random.fold_in(jax.random.fold_in(rng, 6), dim), (blocks,), jnp.float32, least / len(cuts), top_value / len(cuts))
        return jnp.repeat(jnp.exp(steps), shape[dim] // blocks).reshape((-1,) + (1,) * (len(shape) - dim - 1))

    gain = one(*cuts[0])
    for cut in cuts[1:]:
        gain = gain * one(*cut)
    return gain


def shared_out(rng, own, number, rows, amount, top, reach, lean):
    sequence = jax.random.permutation(rng, amount)
    heavy_load, usual = shares(amount, rows * top, reach, lean, True), shares(amount, rows * top, reach, lean, False)
    places = jnp.arange(amount)

    def named(sizes, offset_by):
        used = int((sizes > 0).sum())
        fixed = max(1, used // 4)
        shifted = fixed + (places - fixed + offset_by * (used - fixed)) % max(1, amount - fixed)
        return jnp.zeros((amount,), jnp.int32).at[sequence[jnp.where(places < fixed, places, shifted)]].set(jnp.asarray(sizes, jnp.int32))

    sizes = jnp.where(number % 4 == 0, named(heavy_load, number // 4), named(usual, number - number // 4 - 1))
    mixed = jax.random.permutation(jax.random.fold_in(own, 3), amount)
    donor, receiver = mixed[0:amount // 2 * 2:2], mixed[1:amount // 2 * 2:2]
    margin = jnp.minimum(sizes[donor] - 1, reach - sizes[receiver]) // 2
    margin = jnp.where((donor == sequence[0]) | (receiver == sequence[0]) | (sizes[receiver] == 0), 0, jnp.maximum(margin, 0))
    shifted = jax.random.randint(jax.random.fold_in(own, 4), (amount // 2,), 0, 1 << 20) % (margin + 1)
    sizes = sizes.at[donor].add(-shifted).at[receiver].add(shifted)
    items = jnp.searchsorted(jnp.cumsum(sizes), jnp.arange(rows * top), side="right").astype(jnp.int32)
    listing = items.reshape(top, rows).T
    listing = listing[jax.random.permutation(jax.random.fold_in(own, 1), rows)]
    offset_by = jax.random.randint(jax.random.fold_in(own, 2), (rows, 1), 0, top)
    return jnp.take_along_axis(listing, (jnp.arange(top)[None, :] + offset_by) % top, axis=1)


def shares(count, total, bound, skew, full):
    weights = [(1 << 20) // math.isqrt(standing ** skew) + 1 for standing in range(1, count + 1)]
    largest = bound if full else min(bound, max(-(-total // count), total * weights[0] // sum(weights)))
    least = 1 if total - largest >= count - 1 else 0
    given, spare = [largest] + [least] * (count - 1), total - largest - least * (count - 1)
    while spare > 0:
        free = [i for i in range(1, count) if given[i] < largest] or [i for i in range(1, count) if given[i] < bound]
        whole, budget = sum([weights[i] for i in free]), spare
        for i in free:
            extra = min(bound - given[i], max(1, budget * weights[i] // whole), spare)
            given[i] = given[i] + extra
            spare = spare - extra
    return np.array(given)


def centred(stream_key, shape, scale, bound, split=(), kind=jnp.bfloat16):
    drawn = scale * jax.random.normal(stream_key, shape, jnp.float32)
    if split:
        drawn = drawn * levels(stream_key, shape, split, -0.22, 0.18)
    return jnp.clip(drawn, -bound, bound).astype(kind)


def setup_inputs(seed: int = 0) -> dict:
    splits = jax.random.split(jax.random.key(seed), 8)
    tokens = centred(splits[0], (TOKENS, D), 1.0, 6.0, ((0, 16),))
    out_grad = centred(splits[1], (TOKENS, D), 1.0, 6.0, ((0, 16),))
    route_ids_keys = jax.random.split(jax.random.fold_in(splits[2], 1), TOKENS // TOK_DEV)
    route_ids_turns = jax.random.permutation(jax.random.fold_in(splits[2], 3), TOKENS // TOK_DEV)
    route_ids = jax.vmap(lambda own, number: shared_out(jax.random.fold_in(splits[2], 2), own, number, TOK_DEV, EXPERTS, TOPK, CAP, 2))(route_ids_keys, route_ids_turns).reshape((TOKENS, TOPK))
    route_probs = jnp.clip(jnp.exp(math.log(1.0) - 2.9957323 * jax.random.uniform(splits[3], (TOKENS, TOPK), jnp.float32) ** levels(splits[3], (TOKENS, TOPK), ((0, 16),), -0.2, 0.2)), 0.05, 1.0)
    gate_store = centred(splits[4], (EXPERTS, D, HID), D ** -0.5, 0.125, ((1, 16), (2, 2)))
    up_store = centred(splits[5], (EXPERTS, D, HID), D ** -0.5, 0.125, ((1, 16), (2, 2)))
    down_store = centred(splits[6], (EXPERTS, D, HID), HID ** -0.5, 0.21875, ((1, 16), (2, 2)))
    return {"tokens": tokens, "out_grad": out_grad, "route_ids": route_ids, "route_probs": route_probs, "gate_store": gate_store, "up_store": up_store, "down_store": down_store}


def reference(tokens, out_grad, route_ids, route_probs, gate_store, up_store, down_store):
    top_count = route_ids.shape[1]
    flat_ids = route_ids.reshape(-1)
    flat_probs = route_probs.reshape(-1)
    slot_total = flat_ids.shape[0]
    most_rows = N_EXPERT * CAP

    def per_expert(token_sum, expert):
        slot_list = jnp.nonzero(flat_ids == expert, size=most_rows, fill_value=slot_total)[0].astype(jnp.int32)
        is_valid = slot_list < slot_total
        safe_index = jnp.where(is_valid, slot_list, 0).astype(jnp.int32)
        owner_row = (safe_index // top_count).astype(jnp.int32)
        rows_in = jnp.where(is_valid[:, None], tokens[owner_row], jnp.zeros((), jnp.bfloat16)).astype(jnp.bfloat16)
        slot_scale = jnp.where(is_valid, flat_probs[safe_index], jnp.zeros((), jnp.float32))
        slot_grad = (slot_scale[:, None] * out_grad[owner_row].astype(jnp.float32)).astype(jnp.bfloat16)
        gate_panel = gate_store[expert]
        up_panel = up_store[expert]
        down_panel = down_store[expert]
        gate_pre = jnp.dot(rows_in, gate_panel, preferred_element_type=jnp.float32)
        up_pre = jnp.dot(rows_in, up_panel, preferred_element_type=jnp.float32)
        sigmoid_gate = jax.nn.sigmoid(gate_pre)
        activation = (gate_pre * sigmoid_gate * up_pre).astype(jnp.bfloat16)
        act_grad = jnp.dot(slot_grad, down_panel, preferred_element_type=jnp.float32)
        up_grad = (act_grad * gate_pre * sigmoid_gate).astype(jnp.bfloat16)
        gate_grad = (act_grad * up_pre * sigmoid_gate * (1.0 + gate_pre * (1.0 - sigmoid_gate))).astype(jnp.bfloat16)
        contract = (((0,), (0,)), ((), ()))
        down_part = lax.dot_general(slot_grad, activation, contract, preferred_element_type=jnp.float32)
        gate_part = lax.dot_general(rows_in, gate_grad, contract, preferred_element_type=jnp.float32)
        up_part = lax.dot_general(rows_in, up_grad, contract, preferred_element_type=jnp.float32)
        back_contract = (((1,), (1,)), ((), ()))
        slot_input = (lax.dot_general(gate_grad, gate_panel, back_contract, preferred_element_type=jnp.float32)
                      + lax.dot_general(up_grad, up_panel, back_contract, preferred_element_type=jnp.float32)).astype(jnp.bfloat16)
        added = jnp.where(is_valid[:, None], slot_input.astype(jnp.float32), jnp.zeros((), jnp.float32))
        token_sum = token_sum.at[owner_row].add(added)
        return token_sum, (gate_part.astype(jnp.bfloat16), up_part.astype(jnp.bfloat16), down_part.astype(jnp.bfloat16))

    start_sum = jnp.zeros(tokens.shape, jnp.float32)
    token_sum, grads = lax.scan(per_expert, start_sum, jnp.arange(EXPERTS, dtype=jnp.int32))
    return grads[0], grads[1], grads[2], token_sum.astype(jnp.bfloat16)
```

```python
import jax
import jax.numpy as jnp
from jax import lax
from jax.sharding import PartitionSpec as P


def on_device(tokens, out_grad, route_ids, route_probs, gate_store, up_store, down_store):
    tok_rows, model_width = tokens.shape
    top_count = route_ids.shape[1]
    experts = lax.axis_size("expert")
    capacity = max(2, 9 * tok_rows * top_count // (8 * experts))
    slot_total = tok_rows * top_count
    flat_ids = route_ids.reshape(-1)
    expert_range = jnp.arange(experts, dtype=jnp.int32)
    per_count = jnp.sum((flat_ids[:, None] == expert_range[None, :]).astype(jnp.int32), axis=0)
    offsets = jnp.cumsum(per_count) - per_count
    order = jnp.argsort(flat_ids, stable=True)
    sorted_ids = flat_ids[order]
    sorted_rank = jnp.arange(slot_total, dtype=jnp.int32) - offsets[sorted_ids]
    slot_rank = jnp.zeros((slot_total,), jnp.int32).at[order].set(sorted_rank)
    slot_place = flat_ids * capacity + slot_rank
    source = (
        jnp.full((experts * capacity,), slot_total, jnp.int32)
        .at[slot_place]
        .set(jnp.arange(slot_total, dtype=jnp.int32))
    )
    filled = source < slot_total
    safe_index = jnp.where(filled, source, 0)
    owner_row = safe_index // top_count
    x_slots = jnp.where(filled[:, None], tokens[owner_row], jnp.zeros((), jnp.bfloat16))
    slot_prob = jnp.where(filled, route_probs.reshape(-1)[safe_index], 0.0)
    dy_slots = (slot_prob[:, None] * out_grad[owner_row].astype(jnp.float32)).astype(jnp.bfloat16)
    x_slots = x_slots.reshape(experts, capacity, model_width)
    dy_slots = dy_slots.reshape(experts, capacity, model_width)
    gate_all, up_all, down_all = (
        lax.all_to_all(gate_store, "expert", split_axis=0, concat_axis=1, tiled=True),
        lax.all_to_all(up_store, "expert", split_axis=0, concat_axis=1, tiled=True),
        lax.all_to_all(down_store, "expert", split_axis=0, concat_axis=1, tiled=True),
    )
    gate_panel = gate_all[0]
    up_panel = up_all[0]
    col_width = model_width // lax.axis_size("dp")
    col_start = lax.axis_index("dp") * col_width
    x_part = lax.dynamic_slice_in_dim(x_slots, col_start, col_width, 2)
    dy_part = lax.dynamic_slice_in_dim(dy_slots, col_start, col_width, 2)
    x_sent, dy_sent = (
        lax.all_to_all(x_part, "expert", split_axis=0, concat_axis=0, tiled=True),
        lax.all_to_all(dy_part, "expert", split_axis=0, concat_axis=0, tiled=True),
    )
    x_in, dy_in = (
        lax.all_gather(x_sent, "dp", axis=2, tiled=True),
        lax.all_gather(dy_sent, "dp", axis=2, tiled=True),
    )
    rows_in = x_in.reshape(-1, model_width)
    dy_rows = dy_in.reshape(-1, model_width)
    gate_pre = jnp.dot(rows_in, gate_panel, preferred_element_type=jnp.float32)
    up_pre = jnp.dot(rows_in, up_panel, preferred_element_type=jnp.float32)
    sigmoid_gate = jax.nn.sigmoid(gate_pre)
    activation = (gate_pre * sigmoid_gate * up_pre).astype(jnp.bfloat16)
    down_panel = down_all[0]
    act_grad = jnp.dot(dy_rows, down_panel, preferred_element_type=jnp.float32)
    up_grad = (act_grad * gate_pre * sigmoid_gate).astype(jnp.bfloat16)
    gate_grad = (act_grad * up_pre * sigmoid_gate * (1.0 + gate_pre * (1.0 - sigmoid_gate))).astype(
        jnp.bfloat16
    )
    contract = (((0,), (0,)), ((), ()))
    grad_down = lax.dot_general(
        dy_rows, activation, contract, preferred_element_type=jnp.float32
    ).astype(jnp.bfloat16)
    grad_gate = lax.dot_general(
        rows_in, gate_grad, contract, preferred_element_type=jnp.float32
    ).astype(jnp.bfloat16)
    grad_up = lax.dot_general(
        rows_in, up_grad, contract, preferred_element_type=jnp.float32
    ).astype(jnp.bfloat16)
    back_contract = (((1,), (1,)), ((), ()))
    slot_half = lax.dot_general(
        gate_grad, gate_panel, back_contract, preferred_element_type=jnp.float32
    ) + lax.dot_general(up_grad, up_panel, back_contract, preferred_element_type=jnp.float32)
    summed = lax.psum_scatter(
        slot_half.reshape(experts, capacity, model_width), "dp", scatter_dimension=2, tiled=True
    )
    returned = lax.all_to_all(
        summed.astype(jnp.bfloat16), "expert", split_axis=0, concat_axis=0, tiled=True
    )
    share_width = returned.shape[2]
    slot_values = returned.reshape(experts * capacity, share_width)[slot_place]
    token_share = jnp.sum(
        slot_values.reshape(tok_rows, top_count, share_width).astype(jnp.float32), axis=1
    ).astype(jnp.bfloat16)
    grad_tokens = lax.all_gather(token_share, "dp", axis=1, tiled=True)
    return (grad_gate[None], grad_up[None], grad_down[None], grad_tokens)


def gathered(tokens, out_grad, route_ids, route_probs, gate_store, up_store, down_store):
    tok_rows, model_width = tokens.shape
    experts = lax.axis_size("expert")
    half = tok_rows // lax.axis_size("dp")
    start = lax.axis_index("dp") * half
    both = ("expert", "dp")
    chosen = route_ids[:, :, None] == jnp.arange(experts, dtype=jnp.int32)[None, None, :]
    weight = jnp.sum(jnp.where(chosen, route_probs[:, :, None], 0.0), axis=1)
    weight = lax.all_to_all(weight.T.reshape(experts, tok_rows), "expert", split_axis=0, concat_axis=0, tiled=True)
    weight = weight.reshape(-1, 1)
    x_all = lax.all_gather(lax.dynamic_slice_in_dim(tokens, start, half, 0), both, axis=0, tiled=True)
    g_all = lax.all_gather(lax.dynamic_slice_in_dim(out_grad, start, half, 0), both, axis=0, tiled=True)
    gate_panel, up_panel, down_panel = (
        lax.all_to_all(store, "expert", split_axis=0, concat_axis=1, tiled=True)[0]
        for store in (gate_store, up_store, down_store)
    )
    gate_pre = jnp.dot(x_all, gate_panel, preferred_element_type=jnp.float32)
    up_pre = jnp.dot(x_all, up_panel, preferred_element_type=jnp.float32)
    act_grad = jnp.dot(g_all, down_panel, preferred_element_type=jnp.float32) * weight
    sig = jax.nn.sigmoid(gate_pre)
    activation = (gate_pre * sig * up_pre * weight).astype(jnp.bfloat16)
    up_grad = (act_grad * gate_pre * sig).astype(jnp.bfloat16)
    gate_grad = (act_grad * up_pre * sig * (1.0 + gate_pre * (1.0 - sig))).astype(jnp.bfloat16)
    back = (((1,), (1,)), ((), ()))
    slot_half = lax.dot_general(gate_grad, gate_panel, back, preferred_element_type=jnp.float32) + lax.dot_general(
        up_grad, up_panel, back, preferred_element_type=jnp.float32
    )
    share = lax.psum_scatter(slot_half.astype(jnp.bfloat16), both, scatter_dimension=0, tiled=True)
    grad_tokens = lax.all_gather(share, "dp", axis=0, tiled=True)
    outer = (((0,), (0,)), ((), ()))
    grad_down = lax.dot_general(g_all, activation, outer, preferred_element_type=jnp.float32).astype(jnp.bfloat16)
    grad_gate = lax.dot_general(x_all, gate_grad, outer, preferred_element_type=jnp.float32).astype(jnp.bfloat16)
    grad_up = lax.dot_general(x_all, up_grad, outer, preferred_element_type=jnp.float32).astype(jnp.bfloat16)
    return (grad_gate[None], grad_up[None], grad_down[None], grad_tokens)


def choose(tokens, out_grad, route_ids, *rest):
    if lax.axis_size("expert") <= 2 * route_ids.shape[1]:
        return gathered(tokens, out_grad, route_ids, *rest)
    return on_device(tokens, out_grad, route_ids, *rest)


def solution(mesh):
    return jax.shard_map(
        choose,
        mesh=mesh,
        in_specs=(
            P("expert", None),
            P("expert", None),
            P("expert", None),
            P("expert", None),
            P(None, "expert", "dp"),
            P(None, "expert", "dp"),
            P(None, "expert", "dp"),
        ),
        out_specs=(
            P("expert", None, "dp"),
            P("expert", None, "dp"),
            P("expert", None, "dp"),
            P("expert", None),
        ),
        check_vma=False,
    )
```

```python
import jax
import jax.numpy as jnp
from jax import lax
from jax.sharding import PartitionSpec as P


def joined(own, other):
    first = lax.axis_index("dp") == 0
    return jnp.where(first, jnp.concatenate([own, other], -1), jnp.concatenate([other, own], -1))


def swapped(part):
    return lax.ppermute(part, "dp", [(0, 1), (1, 0)])


def placed(tokens, out_grad, route_ids, route_probs, gate_store, up_store, down_store):
    tok_rows, model_width = tokens.shape
    top_count = route_ids.shape[1]
    experts = lax.axis_size("expert")
    capacity = max(2, 9 * tok_rows * top_count // (8 * experts))
    slots = experts * capacity
    width = model_width // 2
    here = lax.axis_index("dp") * width
    there = width - here
    f32, bf16 = jnp.float32, jnp.bfloat16

    chosen = route_ids[:, :, None] == jnp.arange(experts, dtype=jnp.int32)[None, None, :]
    weight = jnp.sum(jnp.where(chosen, route_probs[:, :, None], 0.0), axis=1)
    named = jnp.any(chosen, axis=1)
    earlier = jnp.arange(tok_rows)[:, None] > jnp.arange(tok_rows)[None, :]
    rank = jnp.dot(earlier.astype(bf16), named.astype(bf16), preferred_element_type=f32)
    rank = jnp.where(named, rank, -1.0)
    hit = rank.T[:, None, :] == jnp.arange(capacity, dtype=f32)[None, :, None]
    slot_prob = jnp.sum(jnp.where(hit, weight.T[:, None, :], 0.0), axis=2)
    place = hit.astype(bf16).reshape(slots, tok_rows)

    x_part = jnp.dot(
        place, lax.dynamic_slice_in_dim(tokens, here, width, 1), preferred_element_type=f32
    ).astype(bf16)
    dy_part = (
        jnp.dot(place, lax.dynamic_slice_in_dim(out_grad, here, width, 1), preferred_element_type=f32)
        * slot_prob.reshape(slots, 1)
    ).astype(bf16)

    def exchange(a):
        return lax.all_to_all(a, "expert", split_axis=0, concat_axis=0, tiled=True)

    def panel(store):
        return lax.all_to_all(store, "expert", split_axis=0, concat_axis=1, tiled=True)[0]

    x_own = exchange(x_part.reshape(experts, capacity, width)).reshape(slots, width)
    gate_panel = panel(gate_store)
    up_panel = panel(up_store)
    dy_own = exchange(dy_part.reshape(experts, capacity, width)).reshape(slots, width)
    down_panel = panel(down_store)
    rows_in = joined(x_own, swapped(x_own))
    dy_rows = joined(dy_own, swapped(dy_own))
    gate_pre = jnp.dot(rows_in, gate_panel, preferred_element_type=f32)
    up_pre = jnp.dot(rows_in, up_panel, preferred_element_type=f32)
    sig = jax.nn.sigmoid(gate_pre)
    activation = (gate_pre * sig * up_pre).astype(bf16)
    act_grad = jnp.dot(dy_rows, down_panel, preferred_element_type=f32)
    up_grad = (act_grad * gate_pre * sig).astype(bf16)
    gate_grad = (act_grad * up_pre * sig * (1.0 + gate_pre * (1.0 - sig))).astype(bf16)
    back = (((1,), (1,)), ((), ()))

    def slot_part(start):
        rows = [lax.dynamic_slice_in_dim(w, start, width, 0) for w in (gate_panel, up_panel)]
        return lax.dot_general(gate_grad, rows[0], back, preferred_element_type=f32) + lax.dot_general(
            up_grad, rows[1], back, preferred_element_type=f32
        )

    arrived = swapped(slot_part(there).astype(bf16))
    summed = (slot_part(here) + arrived.astype(f32)).astype(bf16)
    returned = exchange(summed.reshape(experts, capacity, width)).reshape(slots, width)
    share = lax.dot_general(place, returned, (((0,), (0,)), ((), ())), preferred_element_type=f32).astype(bf16)
    grad_tokens = joined(share, swapped(share))
    outer = (((0,), (0,)), ((), ()))
    grad_down = lax.dot_general(dy_rows, activation, outer, preferred_element_type=f32).astype(bf16)
    grad_gate = lax.dot_general(rows_in, gate_grad, outer, preferred_element_type=f32).astype(bf16)
    grad_up = lax.dot_general(rows_in, up_grad, outer, preferred_element_type=f32).astype(bf16)
    return (grad_gate[None], grad_up[None], grad_down[None], grad_tokens)


def solution(mesh):
    return jax.shard_map(
        placed,
        mesh=mesh,
        in_specs=(
            P("expert", None),
            P("expert", None),
            P("expert", None),
            P("expert", None),
            P(None, "expert", "dp"),
            P(None, "expert", "dp"),
            P(None, "expert", "dp"),
        ),
        out_specs=(
            P("expert", None, "dp"),
            P("expert", None, "dp"),
            P("expert", None, "dp"),
            P("expert", None),
        ),
        check_vma=False,
    )
```
